32 devices in a mesh: ep: 8 (over y, x, core), dp: 4 (over z).
Axes of the slice: x: 2, y: 2, z: 4, core: 2. Of those that a mesh axis runs over, the one named last changes fastest.
Arguments:
- hidden: bfloat16 [8, 1024, 768], P('ep', 'dp'), may hold values from -6 to 6
- cotangent: bfloat16 [8, 1024, 2048], P('ep', 'dp'), may hold values from -0.796875 to 0.796875
- down_weight: bfloat16 [8, 768, 2048], P('ep', 'dp'), may hold values from -0.21875 to 0.21875
- slot_expert: int32 [8], replicated, may hold values from 0 to 127, as said below
- row_counts: int32 [8, 4], P('ep', 'dp'), may hold values from 128 to 256, as said below
Outputs:
- output: bfloat16 [8, 1024, 2048], P('ep', 'dp')
- hidden_grad: bfloat16 [8, 1024, 768], P('ep', 'dp')
- weight_grad: bfloat16 [8, 768, 2048], P('ep', 'dp')
The draws below stay inside these ranges and needn't reach their ends.
Inputs may be any that keep to these rules, and one draw needn't show every extreme that they name: `slot_expert`: equal values form runs of 2 to 4 neighbouring slots, and runs of 2 occur; different runs carry different values. `row_counts`: multiples of 128; some entry equals 256 and some equals 128.
All inputs are finite; a program needn't handle non-finite values.
Results may differ from the reference program's by a relative error of at most 0.012.
Values may be sent and summed in bfloat16 or wider, within the bound.
No kernel may reach another device: no remote copies, remote signals or barrier semaphores. Data moves between devices by JAX's collectives and lax.ppermute only.
A program may use at most 64 MiB of HBM per device.

```python
import jax
import jax.numpy as jnp
import numpy as np
from jax import lax

D = 2048
FF = 768
EXPERTS = 128
CAP = 256
SLOTS = 8
ROWS = 1024
N_EP = 8
N_DP = 4


block_patterns = np.array([[1, 0, 0, 0, 1, 0, 1, 0], [1, 0, 1, 0, 1, 0, 1, 0], [1, 0, 1, 0, 1, 0, 0, 0], [1, 0, 0, 0, 1, 0, 0, 0], [1, 0, 0, 1, 0, 0, 1, 0], [1, 0, 1, 0, 0, 1, 0, 0], [1, 0, 0, 1, 0, 1, 0, 0], [1, 0, 1, 0, 0, 0, 1, 0], [1, 0, 0, 1, 0, 0, 0, 1], [0, 1, 0, 1, 0, 0, 1, 0]], dtype=np.int32)


def draw_slot_expert(key, part):
    blocks_count = N_EP // 8
    middle_block = N_EP // 2 // 8
    picks = jax.random.randint(jax.random.fold_in(key, 11), (blocks_count,), 0, 8)
    picks = picks.at[0].set(0)
    if N_EP % 16 == 0:
        picks = picks.at[middle_block - 1].set(8).at[middle_block].set(9)
    else:
        picks = picks.at[middle_block].set(4)
    begins = jnp.asarray(block_patterns)[picks].reshape(-1)
    group_ids = jnp.cumsum(begins) - 1
    others = 1 + jax.random.permutation(jax.random.fold_in(key, 12), EXPERTS - 2).astype(jnp.int32)
    labels = jnp.concatenate([jnp.array([EXPERTS - 1, 0], dtype=jnp.int32), others])
    return labels[group_ids].astype(jnp.int32)


def draw_row_counts(key, part):
    multiples = jax.random.randint(jax.random.fold_in(key, 21), (N_EP, N_DP), 1, CAP // 128 + 1)
    counts_drawn = 128 * multiples
    counts_drawn = counts_drawn.at[0, 0].set(CAP).at[0, 1].set(128)
    return counts_drawn.astype(jnp.int32)


def block_levels(own_key, extent, shards, low, largest):
    gain = 1.0
    for dim, shards_of in shards:
        draws = jax.random.uniform(jax.random.fold_in(jax.random.fold_in(own_key, 6), dim), (shards_of,), jnp.float32, low / len(shards), largest / len(shards))
        gain = gain * jnp.repeat(jnp.exp(draws), extent[dim] // shards_of).reshape((-1,) + (1,) * (len(extent) - 1 - dim))
    return gain


def normal_values(stream_key, extent, width, reach, split=(), held_as=jnp.bfloat16):
    loudness = block_levels(stream_key, extent, split, -0.22, 0.18) if split else 1.0
    values = jax.random.normal(stream_key, extent, jnp.float32) * width * loudness
    return jnp.minimum(jnp.maximum(values, -reach), reach).astype(held_as)


def setup_inputs(seed: int = 0) -> dict:
    key_of = jax.random.split(jax.random.key(seed), 6)
    hidden = normal_values(key_of[0], (SLOTS, ROWS, FF), 1.0, 6.0, ((0, 8), (1, 4)))
    cotangent = normal_values(key_of[1], (SLOTS, ROWS, D), 0.1, 0.796875, ((0, 8), (1, 4)))
    down_weight = normal_values(key_of[2], (SLOTS, FF, D), FF ** -0.5, 0.21875, ((0, 8), (1, 4)))
    slot_expert = draw_slot_expert(jax.random.fold_in(key_of[5], 71), 0)
    row_counts = draw_row_counts(jax.random.fold_in(key_of[5], 71), 0)
    return {"hidden": hidden, "cotangent": cotangent, "down_weight": down_weight, "slot_expert": slot_expert, "row_counts": row_counts}


def reference(hidden, cotangent, down_weight, slot_expert, row_counts):
    total_slots = slot_expert.shape[0]
    places = jnp.arange(total_slots, dtype=jnp.int32)
    earlier = jnp.concatenate([slot_expert[:1] - 1, slot_expert[:-1]])
    begins = slot_expert != earlier
    group_ids = (jnp.cumsum(begins.astype(jnp.int32)) - 1).astype(jnp.int32)
    owners = jnp.min(jnp.where(group_ids[None, :] == group_ids[:, None], places[None, :], total_slots), axis=1).astype(jnp.int32)
    capacity = hidden.shape[1] // N_DP
    positions = jnp.arange(capacity, dtype=jnp.int32)
    live_rows = (positions[None, None, :] < row_counts[:, :, None]).reshape(total_slots, N_DP * capacity, 1)
    masked_hidden = jnp.where(live_rows, hidden, jnp.zeros((), hidden.dtype))
    masked_grads = jnp.where(live_rows, cotangent, jnp.zeros((), cotangent.dtype))

    def per_slot(slot_index):
        owner_index = lax.dynamic_index_in_dim(owners, slot_index, 0, keepdims=False)
        weight = lax.dynamic_index_in_dim(down_weight, owner_index, 0, keepdims=False)
        rows_hidden = lax.dynamic_index_in_dim(masked_hidden, slot_index, 0, keepdims=False)
        rows_grads = lax.dynamic_index_in_dim(masked_grads, slot_index, 0, keepdims=False)
        outputs = jnp.dot(rows_hidden, weight, preferred_element_type=jnp.float32).astype(jnp.bfloat16)
        input_grads = jnp.dot(rows_grads, weight.T, preferred_element_type=jnp.float32).astype(jnp.bfloat16)
        split_hidden = rows_hidden.reshape(N_DP, capacity, -1).astype(jnp.float32)
        split_grads = rows_grads.reshape(N_DP, capacity, -1).astype(jnp.float32)
        partials = jnp.einsum("ncf,ncd->nfd", split_hidden, split_grads).astype(jnp.bfloat16)
        partials = lax.optimization_barrier(partials)
        replica_sum = jnp.sum(partials.astype(jnp.float32), axis=0).astype(jnp.bfloat16)
        return outputs, input_grads, replica_sum

    outputs, input_grads, replica_sums = lax.map(per_slot, places)
    replica_sums = lax.optimization_barrier(replica_sums)
    group_totals = jax.ops.segment_sum(replica_sums.astype(jnp.float32), group_ids, num_segments=total_slots)
    weight_grad = group_totals[group_ids].astype(jnp.bfloat16)
    return outputs, input_grads, weight_grad
```

```python
import jax
import jax.numpy as jnp
from jax import lax
from jax.sharding import PartitionSpec as P

BF16 = jnp.bfloat16
F32 = jnp.float32


def make_body(n_ep, n_dp):
    assert n_dp == 4 and n_ep % 2 == 0
    both = ("ep", "dp")
    core_pairs = [(s, s ^ 1) for s in range(n_ep)]
    help_pairs = [(s, s + 1 if s % 2 else s - 1) for s in range(2, n_ep - 2)]
    back_pairs = [(b, a) for a, b in help_pairs]
    right_two = [(s, s + 2) for s in range(n_ep - 2)]
    left_two = [(s + 2, s) for s in range(n_ep - 2)]
    right_four_weight = [(s - 4, s) for s in range(6, n_ep - 2, 2)]
    right_four_grad = [(s - 4, s) for s in range(7, n_ep - 2, 2)]
    left_four_grad = [(s + 4, s) for s in range(2, n_ep - 7, 2)]
    side_pairs = [(0, 1), (1, 0), (2, 3), (3, 2)]
    middle_pairs = []
    for s in range(n_ep):
        for z in range(n_dp):
            t, w = (s, z ^ 3) if z in (1, 2) else (s ^ 1, z)
            middle_pairs.append((s * n_dp + z, t * n_dp + w))

    def core(x):
        return lax.ppermute(x, "ep", core_pairs)

    def shift(x, pairs):
        return lax.ppermute(x, "ep", pairs) if pairs else jnp.zeros_like(x)

    def side(x):
        return lax.ppermute(x, "dp", side_pairs)

    def middle(x):
        return lax.ppermute(x, both, middle_pairs)

    def plus(a, b):
        return (a.astype(F32) + b.astype(F32)).astype(BF16)

    def body(hidden, cotangent, down_weight, slot_expert, row_counts):
        s = lax.axis_index("ep")
        z = lax.axis_index("dp")
        odd = (s % 2) == 1
        is_middle = (z == 1) | (z == 2)
        capacity, units = hidden.shape[1:]
        quarter, features = down_weight.shape[1:]
        half = features // 2
        pad = jnp.full((4,), -1, jnp.int32)
        window = lax.dynamic_slice(jnp.concatenate([pad, slot_expert, pad]), (s,), (9,))
        e = [window[k] for k in range(9)]
        own = e[4]
        eq = {d: e[4 + d] == own for d in (-3, -2, -1, 1, 2, 3)}
        with_partner = jnp.where(odd, eq[-1], eq[1])
        helps = jnp.where(odd, eq[1] & (e[6] != own), eq[-1] & (e[2] != own))

        def low(x):
            return jnp.where(odd, x[:, half:], x[:, :half])

        def high(x):
            return jnp.where(odd, x[:, :half], x[:, half:])

        stored = down_weight[0]
        own_part = low(stored)
        partner_part = core(high(stored))
        export = jnp.where(with_partner != odd, own_part, partner_part)
        came = shift(export, right_two)
        if right_four_weight:
            came = jnp.where(eq[-3] & ~odd, shift(export, right_four_weight), came)
        unit = jnp.where(
            ~eq[-1], own_part, jnp.where(odd & ~eq[-2], partner_part, came)
        )

        live = (lax.iota(jnp.int32, capacity) < row_counts[0, 0])[:, None]
        zero = jnp.zeros((), BF16)
        h = jnp.where(live, hidden[0], zero)
        c = jnp.where(live, cotangent[0], zero)
        sent = jnp.concatenate([h, high(c)], axis=1)
        from_core = core(sent)
        from_next = shift(sent, help_pairs)
        from_core = jnp.where(with_partner, from_core, zero)
        from_next = jnp.where(helps, from_next, zero)
        hs = jnp.concatenate([h, from_core[:, :units], from_next[:, :units]], axis=0)
        cs = jnp.concatenate([low(c), from_core[:, units:], from_next[:, units:]], axis=0)
        grads = lax.dot_general(
            hs, cs, (((0,), (0,)), ((), ())), preferred_element_type=F32
        ).astype(BF16)

        def term(k):
            return lax.dynamic_slice(grads, ((z ^ k) * quarter, 0), (quarter, half))

        a1 = side(unit)
        m1 = middle(unit)
        a2 = side(jnp.where(is_middle, m1, term(3)))
        m2 = middle(a1)
        a3 = side(jnp.where(is_middle, m2, term(2)))
        m3 = middle(plus(a2, term(2)))
        a4 = side(jnp.where(is_middle, plus(m3, term(1)), term(1)))
        m4 = middle(plus(a3, term(3)))

        by_xor = [unit, a1, jnp.where(is_middle, m2, a2), jnp.where(is_middle, m1, a3)]
        flip1, flip2 = (z % 2) == 1, z >= 2
        x = [jnp.where(flip1, by_xor[k ^ 1], by_xor[k]) for k in range(4)]
        x = [jnp.where(flip2, x[k ^ 2], x[k]) for k in range(4)]
        weight = jnp.concatenate(x, axis=0)
        outs = jnp.dot(hs, weight, preferred_element_type=F32).astype(BF16)
        hgs = lax.dot_general(
            cs, weight, (((1,), (1,)), ((), ())), preferred_element_type=F32
        )
        hgb = hgs[capacity:].astype(BF16)
        made = jnp.concatenate([outs[capacity:], hgb], axis=1)
        back = jnp.where(
            with_partner, core(made[:capacity]), shift(made[capacity:], back_pairs)
        )
        o, q = outs[:capacity], back[:, :half]
        output = jnp.concatenate([jnp.where(odd, q, o), jnp.where(odd, o, q)], axis=1)
        hidden_grad = (hgs[:capacity] + back[:, half:].astype(F32)).astype(BF16)

        total = a4.astype(F32) + term(0).astype(F32)
        total = total + jnp.where(is_middle, m4.astype(F32), 0.0)
        held = total.astype(BF16)
        left = shift(held, right_two).astype(F32)
        right = shift(held, left_two).astype(F32)
        group = total + jnp.where(eq[-2], left, 0.0) + jnp.where(eq[2], right, 0.0)
        other = jnp.where(odd, left, right)
        if right_four_grad:
            far = jnp.where(odd, shift(held, right_four_grad), shift(held, left_four_grad))
            far_in = jnp.where(odd, e[0] == e[3], e[8] == e[5])
            other = other + jnp.where(far_in, far.astype(F32), 0.0)
        group = group.astype(BF16)
        g = core(jnp.where(with_partner, group, other.astype(BF16)))
        weight_grad = jnp.concatenate(
            [jnp.where(odd, g, group), jnp.where(odd, group, g)], axis=1
        )
        return output[None], hidden_grad[None], weight_grad[None]

    return body


def solution(mesh):
    spec = P("ep", "dp", None)
    return jax.shard_map(
        make_body(mesh.shape["ep"], mesh.shape["dp"]),
        mesh=mesh,
        in_specs=(spec, spec, spec, P(), P("ep", "dp")),
        out_specs=(spec, spec, spec),
        check_vma=False,
    )
```

```python
import jax
import jax.numpy as jnp
from jax import lax
from jax.sharding import PartitionSpec as P

BF16 = jnp.bfloat16
F32 = jnp.float32


def make_body(n_ep, n_dp):
    assert n_dp == 4 and n_ep % 2 == 0
    both = ("ep", "dp")
    core_pairs = [(s, s ^ 1) for s in range(n_ep)]
    help_pairs = [(s, s + 1 if s % 2 else s - 1) for s in range(2, n_ep - 2)]
    back_pairs = [(b, a) for a, b in help_pairs]
    far = [(a, b) for a, b in help_pairs if {a % 8, b % 8} == {3, 4}]
    relays = {a ^ 5 for a, b in far}
    near = [(a, b) for a, b in help_pairs if (a, b) not in far]
    hop_one = [(a, a ^ 5) for a, b in far] + [p for p in near if p[0] in relays]
    hop_two = [(a ^ 5, b) for a, b in far] + [p for p in near if p[0] not in relays]
    hop_one_ends = [b for a, b in near if a in relays]
    right_two = [(s, s + 2) for s in range(n_ep - 2)]
    left_two = [(s + 2, s) for s in range(n_ep - 2)]
    right_four_weight = [(s - 4, s) for s in range(6, n_ep - 2, 2)]
    right_four_grad = [(s - 4, s) for s in range(7, n_ep - 2, 2)]
    left_four_grad = [(s + 4, s) for s in range(2, n_ep - 7, 2)]
    side_pairs = [(0, 1), (1, 0), (2, 3), (3, 2)]
    middle_pairs = []
    for s in range(n_ep):
        for z in range(n_dp):
            t, w = (s, z ^ 3) if z in (1, 2) else (s ^ 1, z)
            middle_pairs.append((s * n_dp + z, t * n_dp + w))

    def core(x):
        return lax.ppermute(x, "ep", core_pairs)

    def shift(x, pairs):
        return lax.ppermute(x, "ep", pairs) if pairs else jnp.zeros_like(x)

    def side(x):
        return lax.ppermute(x, "dp", side_pairs)

    def middle(x):
        return lax.ppermute(x, both, middle_pairs)

    def plus(a, b):
        return (a.astype(F32) + b.astype(F32)).astype(BF16)

    def body(hidden, cotangent, down_weight, slot_expert, row_counts):
        s = lax.axis_index("ep")
        z = lax.axis_index("dp")
        odd = (s % 2) == 1
        is_middle = (z == 1) | (z == 2)
        capacity, units = hidden.shape[1:]
        quarter, features = down_weight.shape[1:]
        half = features // 2
        pad = jnp.full((4,), -1, jnp.int32)
        window = lax.dynamic_slice(jnp.concatenate([pad, slot_expert, pad]), (s,), (9,))
        e = [window[k] for k in range(9)]
        own = e[4]
        eq = {d: e[4 + d] == own for d in (-3, -2, -1, 1, 2, 3)}
        with_partner = jnp.where(odd, eq[-1], eq[1])
        helps = jnp.where(odd, eq[1] & (e[6] != own), eq[-1] & (e[2] != own))

        own_at = (s % 2) * half

        def low(x):
            return lax.dynamic_slice(x, (0, own_at), (x.shape[0], half))

        def high(x):
            return lax.dynamic_slice(x, (0, half - own_at), (x.shape[0], half))

        stored = down_weight[0]
        own_part = low(stored)
        partner_part = core(high(stored))
        export = jnp.where(with_partner != odd, own_part, partner_part)
        came = shift(export, right_two)
        if right_four_weight:
            came = jnp.where(eq[-3] & ~odd, shift(export, right_four_weight), came)
        unit = jnp.where(
            ~eq[-1], own_part, jnp.where(odd & ~eq[-2], partner_part, came)
        )

        live = (lax.iota(jnp.int32, capacity) < row_counts[0, 0])[:, None]
        zero = jnp.zeros((), BF16)
        h = jnp.where(live, hidden[0], zero)
        c = jnp.where(live, cotangent[0], zero)
        sent = jnp.concatenate([h, high(c)], axis=1)
        from_core = core(sent)
        is_relay = jnp.isin(s, jnp.array(sorted(relays), jnp.int32)) if relays else False
        first = shift(sent, hop_one)
        from_next = shift(jnp.where(is_relay, first, sent), hop_two)
        if hop_one_ends:
            by_one = jnp.isin(s, jnp.array(hop_one_ends, jnp.int32))
            from_next = jnp.where(by_one, first, from_next)
        hs = jnp.concatenate([h, from_core[:, :units], from_next[:, :units]], axis=0)
        cs = jnp.concatenate(
            [
                low(c),
                jnp.where(with_partner, from_core[:, units:], zero),
                jnp.where(helps, from_next[:, units:], zero),
            ],
            axis=0,
        )
        grads = lax.dot_general(
            hs, cs, (((0,), (0,)), ((), ())), preferred_element_type=F32
        ).astype(BF16)

        terms = lax.optimization_barrier(
            [
                lax.dynamic_slice(grads, ((z ^ k) * quarter, 0), (quarter, half))
                for k in range(4)
            ]
        )

        def term(k):
            return terms[k]

        a1 = side(unit)
        m1 = middle(unit)
        a2 = side(jnp.where(is_middle, m1, term(3)))
        m2 = middle(a1)
        a3 = side(jnp.where(is_middle, m2, term(2)))
        m3 = middle(plus(a2, term(2)))
        a4 = side(jnp.where(is_middle, plus(m3, term(1)), term(1)))
        m4 = middle(plus(a3, term(3)))

        by_xor = [unit, a1, jnp.where(is_middle, m2, a2), jnp.where(is_middle, m1, a3)]
        flip1, flip2 = (z % 2) == 1, z >= 2
        x = [jnp.where(flip1, by_xor[k ^ 1], by_xor[k]) for k in range(4)]
        x = [jnp.where(flip2, x[k ^ 2], x[k]) for k in range(4)]
        weight = jnp.concatenate(x, axis=0)
        outs = jnp.dot(hs, weight, preferred_element_type=F32).astype(BF16)
        hgs = lax.dot_general(
            cs, weight, (((1,), (1,)), ((), ())), preferred_element_type=F32
        )
        hgb = hgs[capacity:].astype(BF16)
        made = jnp.concatenate([outs[capacity:], hgb], axis=1)
        back = jnp.where(
            with_partner, core(made[:capacity]), shift(made[capacity:], back_pairs)
        )
        o, q = outs[:capacity], back[:, :half]
        output = jnp.concatenate([jnp.where(odd, q, o), jnp.where(odd, o, q)], axis=1)
        hidden_grad = (hgs[:capacity] + back[:, half:].astype(F32)).astype(BF16)

        total = a4.astype(F32) + term(0).astype(F32)
        total = total + jnp.where(is_middle, m4.astype(F32), 0.0)
        held = total.astype(BF16)
        left = shift(held, right_two).astype(F32)
        right = shift(held, left_two).astype(F32)
        group = total + jnp.where(eq[-2], left, 0.0) + jnp.where(eq[2], right, 0.0)
        other = jnp.where(odd, left, right)
        if right_four_grad:
            far = jnp.where(odd, shift(held, right_four_grad), shift(held, left_four_grad))
            far_in = jnp.where(odd, e[0] == e[3], e[8] == e[5])
            other = other + jnp.where(far_in, far.astype(F32), 0.0)
        group = group.astype(BF16)
        g = core(jnp.where(with_partner, group, other.astype(BF16)))
        weight_grad = jnp.concatenate(
            [jnp.where(odd, g, group), jnp.where(odd, group, g)], axis=1
        )
        return output[None], hidden_grad[None], weight_grad[None]

    return body


def solution(mesh):
    spec = P("ep", "dp", None)
    return jax.shard_map(
        make_body(mesh.shape["ep"], mesh.shape["dp"]),
        mesh=mesh,
        in_specs=(spec, spec, spec, P(), P("ep", "dp")),
        out_specs=(spec, spec, spec),
        check_vma=False,
    )
```

```python
import jax
import jax.numpy as jnp
from jax import lax
from jax.experimental import pallas as pl
from jax.experimental.pallas import tpu as pltpu
from jax.sharding import PartitionSpec as P


BF16 = jnp.bfloat16
F32 = jnp.float32
BLOCK = 128
FLAGS = (
    "odd", "z", "count", "partner", "helps", "begins", "before_two",
    "after_two", "export_own", "far_weight", "far_grad", "relay", "by_one",
)


def local_kernel(kernel, out_shapes, scratch=(), flops=0, moved=0, mib=8):
    def call(flags, *arrays):
        vmem = pl.BlockSpec(memory_space=pltpu.VMEM)
        return pl.pallas_call(
            kernel,
            out_shape=out_shapes,
            in_specs=[pl.BlockSpec(memory_space=pltpu.SMEM)] + [vmem] * len(arrays),
            out_specs=jax.tree.map(lambda _: vmem, out_shapes),
            scratch_shapes=list(scratch),
            compiler_params=pltpu.CompilerParams(vmem_limit_bytes=mib << 20),
            cost_estimate=pl.CostEstimate(
                flops=flops, bytes_accessed=moved, transcendentals=0
            ),
        )(flags, *arrays)

    return call


def flag(ref, name):
    return ref[FLAGS.index(name)]


def cols(at, size):
    return pl.ds(pl.multiple_of(at, BLOCK), size)


def copy_live(flags, rows, store):
    for r in range(0, rows, BLOCK):
        store(slice(r, r + BLOCK), r < flag(flags, "count"))


def masked(keep, x):
    return jnp.where(keep, x, jnp.zeros_like(x))


def pack_kernel(flags, hid, cot, sent_h, sent_c):
    half = cot.shape[1] // 2
    other = cols((1 - flag(flags, "odd")) * half, half)

    def store(r, live):
        sent_h[r, :] = masked(live, hid[r, :])
        sent_c[r, :] = masked(live, cot[r, other])

    copy_live(flags, hid.shape[0], store)


def choose_kernel(name):
    def kernel(flags, yes, no, out):
        @pl.when(flag(flags, name) != 0)
        def _():
            out[...] = yes[...]

        @pl.when(flag(flags, name) == 0)
        def _():
            out[...] = no[...]

    return kernel


def export_kernel(flags, stored, partner_part, out):
    half = out.shape[1]

    @pl.when(flag(flags, "export_own") != 0)
    def _():
        out[...] = stored[:, cols(flag(flags, "odd") * half, half)]

    @pl.when(flag(flags, "export_own") == 0)
    def _():
        out[...] = partner_part[...]


def unit_kernel(flags, stored, partner_part, came, out):
    half = out.shape[1]
    begins = flag(flags, "begins") != 0
    paired = (flag(flags, "odd") != 0) & (flag(flags, "before_two") == 0)

    @pl.when(begins)
    def _():
        out[...] = stored[:, cols(flag(flags, "odd") * half, half)]

    @pl.when(jnp.logical_not(begins) & paired)
    def _():
        out[...] = partner_part[...]

    @pl.when(jnp.logical_not(begins | paired))
    def _():
        out[...] = came[...]


def grad_kernel(flags, hid, cot, core_h, core_c, near_h, near_c, t0, t1, t2, t3, ht, cs):
    rows, units = hid.shape
    half = cot.shape[1] // 2
    own = cols(flag(flags, "odd") * half, half)

    def store(r, live):
        cs[r, :] = masked(live, cot[r, own])

    copy_live(flags, rows, store)
    cs[rows : 2 * rows, :] = masked(flag(flags, "partner") != 0, core_c[...])
    cs[2 * rows :, :] = masked(flag(flags, "helps") != 0, near_c[...])
    ht[:, :rows] = hid[...].T
    ht[:, rows : 2 * rows] = core_h[...].T
    ht[:, 2 * rows :] = near_h[...].T
    z = flag(flags, "z")
    quarter = units // 4
    for k, term in enumerate((t0, t1, t2, t3)):
        at = pl.multiple_of((z ^ k) * quarter, 16)
        term[...] = jnp.dot(
            ht[pl.ds(at, quarter), :], cs[...], preferred_element_type=F32
        ).astype(BF16)


def sum_kernel(flags, held, left, right, *rest):
    far, own, other = rest[:-2], rest[-2], rest[-1]
    none = jnp.zeros((), F32)

    def add(x, keep):
        return jnp.where(keep, x[...].astype(F32), none)

    total = held[...].astype(F32) + add(left, flag(flags, "before_two") != 0)
    own[...] = (total + add(right, flag(flags, "after_two") != 0)).astype(BF16)

    @pl.when(flag(flags, "partner") != 0)
    def _():
        other[...] = own[...]

    @pl.when(flag(flags, "partner") == 0)
    def _():
        odd = flag(flags, "odd") != 0
        theirs = jnp.where(odd, left[...].astype(F32), right[...].astype(F32))
        if far:
            more = jnp.where(odd, far[0][...].astype(F32), far[1][...].astype(F32))
            theirs = theirs + jnp.where(flag(flags, "far_grad") != 0, more, none)
        other[...] = theirs.astype(BF16)


def forward_kernel(flags, hid, cot, core_h, core_c, near_h, near_c, u, a1, m1, a2, m2, a3,
                   out, hg, to_core, to_near, weight):
    rows, units = hid.shape
    half = cot.shape[1] // 2
    z = flag(flags, "z")
    middle = (z == 1) | (z == 2)
    quarter = units // 4

    def place(k, value):
        at = pl.multiple_of((z ^ k) * quarter, 16)
        weight[pl.ds(at, quarter), :] = value

    place(0, u[...])
    place(1, a1[...])

    @pl.when(middle)
    def _():
        place(2, m2[...])
        place(3, m1[...])

    @pl.when(jnp.logical_not(middle))
    def _():
        place(2, a2[...])
        place(3, a3[...])

    own = cols(flag(flags, "odd") * half, half)
    w = weight[...]

    def products(h, c):
        o = jnp.dot(h, w, preferred_element_type=F32)
        g = lax.dot_general(c, w, (((1,), (1,)), ((), ())), preferred_element_type=F32)
        return o, g

    def own_rows(r, live):
        o, g = products(masked(live, hid[r, :]), masked(live, cot[r, own]))
        out[r, :] = o.astype(BF16)
        hg[r, :] = g

    copy_live(flags, rows, own_rows)
    for h, c, dst in ((core_h, core_c, to_core), (near_h, near_c, to_near)):
        o, g = products(h[...], c[...])
        dst[:, :half] = o.astype(BF16)
        dst[:, half:] = g.astype(BF16)


def output_kernel(flags, out, hg, core, near, output, hidden_grad):
    half = out.shape[1]
    odd = flag(flags, "odd")
    output[:, cols(odd * half, half)] = out[...]

    def finish(back):
        output[:, cols((1 - odd) * half, half)] = back[:, :half]
        hidden_grad[...] = (hg[...] + back[:, half:].astype(F32)).astype(BF16)

    @pl.when(flag(flags, "partner") != 0)
    def _():
        finish(core)

    @pl.when(flag(flags, "partner") == 0)
    def _():
        finish(near)


def join_kernel(flags, own, other, whole):
    half = own.shape[1]
    odd = flag(flags, "odd")
    whole[:, cols(odd * half, half)] = own[...]
    whole[:, cols((1 - odd) * half, half)] = other[...]


def make_body(n_ep, n_dp):
    assert n_dp == 4 and n_ep % 2 == 0
    both = ("ep", "dp")
    core_pairs = [(s, s ^ 1) for s in range(n_ep)]
    help_pairs = [(s, s + 1 if s % 2 else s - 1) for s in range(2, n_ep - 2)]
    back_pairs = [(b, a) for a, b in help_pairs]
    far = [(a, b) for a, b in help_pairs if {a % 8, b % 8} == {3, 4}]
    relays = {a ^ 5 for a, b in far}
    near = [(a, b) for a, b in help_pairs if (a, b) not in far]
    hop_one = [(a, a ^ 5) for a, b in far] + [p for p in near if p[0] in relays]
    hop_two = [(a ^ 5, b) for a, b in far] + [p for p in near if p[0] not in relays]
    by_one = {b for a, b in near if a in relays}
    right_two = [(s, s + 2) for s in range(n_ep - 2)]
    left_two = [(s + 2, s) for s in range(n_ep - 2)]
    right_four_weight = [(s - 4, s) for s in range(6, n_ep - 2, 2)]
    right_four_grad = [(s - 4, s) for s in range(7, n_ep - 2, 2)]
    left_four_grad = [(s + 4, s) for s in range(2, n_ep - 7, 2)]
    side_pairs = [(0, 1), (1, 0), (2, 3), (3, 2)]
    middle_pairs = []
    for s in range(n_ep):
        for z in range(n_dp):
            t, w = (s, z ^ 3) if z in (1, 2) else (s ^ 1, z)
            middle_pairs.append((s * n_dp + z, t * n_dp + w))

    def permute(x, axes, pairs):
        return lax.ppermute(x, axes, pairs) if pairs else jnp.zeros_like(x)

    def core(x):
        return permute(x, "ep", core_pairs)

    def shift(x, pairs):
        return permute(x, "ep", pairs)

    def side(x):
        return permute(x, "dp", side_pairs)

    def middle(x):
        return permute(x, both, middle_pairs)

    def plus(a, b):
        return (a.astype(F32) + b.astype(F32)).astype(BF16)

    def make_flags(slot_expert, count, s, z):
        places = lax.iota(jnp.int32, n_ep)
        odd = places % 2 == 1
        padded = jnp.pad(slot_expert, 4, constant_values=-1)
        e = {d: padded[4 + d : 4 + d + n_ep] for d in range(-4, 5)}
        eq = {d: e[d] == e[0] for d in e}
        partner = jnp.where(odd, eq[-1], eq[1])

        def among(members):
            found = places < 0
            for m in sorted(members):
                found = found | (places == m)
            return found

        rows = {
            "odd": odd,
            "z": z + 0 * places,
            "count": count + 0 * places,
            "partner": partner,
            "helps": jnp.where(odd, eq[1] & ~eq[2], eq[-1] & ~eq[-2]),
            "begins": ~eq[-1],
            "before_two": eq[-2],
            "after_two": eq[2],
            "export_own": partner != odd,
            "far_weight": eq[-3] & ~odd,
            "far_grad": jnp.where(odd, e[-4] == e[-1], e[4] == e[1]),
            "relay": among(relays),
            "by_one": among(by_one),
        }
        table = jnp.stack([rows[name].astype(jnp.int32) for name in FLAGS])
        return jnp.sum(jnp.where(places == s, table, 0), axis=1)

    def compute(hidden, cotangent, down_weight, slot_expert, row_counts):
        s = lax.axis_index("ep")
        z = lax.axis_index("dp")
        is_middle = (z == 1) | (z == 2)
        hid, cot, stored = hidden[0], cotangent[0], down_weight[0]
        capacity, units = hid.shape
        quarter, features = stored.shape
        half = features // 2
        flags = make_flags(slot_expert, row_counts[0, 0], s, z)

        def is_set(name):
            return flags[FLAGS.index(name)] != 0

        own_at = (s % 2) * half

        other_part = lax.dynamic_slice(stored, (0, half - own_at), (quarter, half))
        other_part, hid, cot = lax.optimization_barrier((other_part, hid, cot))
        own_part = lax.dynamic_slice(stored, (0, own_at), (quarter, half))
        piece = jax.ShapeDtypeStruct((quarter, half), BF16)
        h_piece = jax.ShapeDtypeStruct((capacity, units), BF16)
        c_piece = jax.ShapeDtypeStruct((capacity, half), BF16)
        packed = jax.ShapeDtypeStruct((capacity, units + half), BF16)
        wide = units + half
        small = 6 * quarter * half

        partner_part = core(other_part)
        export = local_kernel(export_kernel, piece, moved=small)(
            flags, stored, partner_part
        )
        came = shift(export, right_two)
        if right_four_weight:
            more = shift(export, right_four_weight)
            came = jnp.where(is_set("far_weight"), more, came)
        unit = local_kernel(unit_kernel, piece, moved=small)(
            flags, stored, partner_part, came
        )

        sent_h, sent_c = local_kernel(
            pack_kernel, [h_piece, c_piece], moved=4 * capacity * wide
        )(flags, hid, cot)

        def to_neighbour(x):
            first = shift(x, hop_one)
            passed = local_kernel(choose_kernel("relay"), x, moved=4 * x.size)(
                flags, first, x
            )
            arrived = shift(passed, hop_two)
            if by_one:
                arrived = jnp.where(is_set("by_one"), first, arrived)
            return arrived

        near = [to_neighbour(sent_h), to_neighbour(sent_c)]
        from_core = [core(sent_h), core(sent_c)]
        terms = local_kernel(
            grad_kernel,
            [piece] * 4,
            [
                pltpu.VMEM((units, 3 * capacity), BF16),
                pltpu.VMEM((3 * capacity, half), BF16),
            ],
            flops=6 * capacity * units * half,
            moved=2 * units * half + 6 * capacity * wide,
            mib=16,
        )(flags, hid, cot, *from_core, *near)

        a1 = side(unit)
        m1 = middle(unit)
        a2 = side(jnp.where(is_middle, m1, terms[3]))
        m2 = middle(a1)
        a3 = side(jnp.where(is_middle, m2, terms[2]))
        m3 = middle(plus(a2, terms[2]))
        last_side = jnp.where(is_middle, plus(m3, terms[1]), terms[1])
        last_middle = plus(a3, terms[3])
        last_side, last_middle, unit = lax.optimization_barrier(
            (last_side, last_middle, unit)
        )
        a4 = side(last_side)
        m4 = middle(last_middle)

        out, hg, to_core, to_next = local_kernel(
            forward_kernel,
            [
                jax.ShapeDtypeStruct((capacity, half), BF16),
                jax.ShapeDtypeStruct((capacity, units), F32),
                packed,
                packed,
            ],
            [pltpu.VMEM((units, half), BF16)],
            flops=12 * capacity * units * half,
            moved=2 * units * half + 12 * capacity * wide,
            mib=24,
        )(flags, hid, cot, *from_core, *near, unit, a1, m1, a2, m2, a3)
        a4, m4, to_core, to_next = lax.optimization_barrier((a4, m4, to_core, to_next))
        output, hidden_grad = local_kernel(
            output_kernel,
            [
                jax.ShapeDtypeStruct((capacity, features), BF16),
                jax.ShapeDtypeStruct((capacity, units), BF16),
            ],
            moved=8 * capacity * wide,
        )(flags, out, hg, core(to_core), shift(to_next, back_pairs))

        total = a4.astype(F32) + terms[0].astype(F32)
        total = total + jnp.where(is_middle, m4.astype(F32), 0.0)
        held = total.astype(BF16)
        arrived = [shift(held, right_two), shift(held, left_two)]
        if right_four_grad:
            arrived.append(shift(held, right_four_grad))
            arrived.append(shift(held, left_four_grad))
        group, other = local_kernel(sum_kernel, [piece, piece], moved=2 * small)(
            flags, held, *arrived
        )
        g = core(other)
        weight_grad = local_kernel(
            join_kernel,
            jax.ShapeDtypeStruct((quarter, features), BF16),
            moved=4 * quarter * features,
        )(flags, group, g)
        return output[None], hidden_grad[None], weight_grad[None]

    return compute


def solution(mesh):
    spec = P("ep", "dp", None)
    return jax.shard_map(
        make_body(mesh.shape["ep"], mesh.shape["dp"]),
        mesh=mesh,
        in_specs=(spec, spec, spec, P(), P("ep", "dp")),
        out_specs=(spec, spec, spec),
        check_vma=False,
    )
```

```python
import jax
import jax.numpy as jnp
from jax import lax
from jax.experimental import pallas as pl
from jax.experimental.pallas import tpu as pltpu
from jax.sharding import PartitionSpec as P


BF16 = jnp.bfloat16
F32 = jnp.float32
BLOCK = 128
FLAGS = (
    "odd", "z", "count", "partner", "helps", "begins", "before_two",
    "after_two", "export_own", "far_weight", "far_grad", "relay", "by_one", "place",
)


def local_kernel(kernel, out_shapes, scratch=(), flops=0, moved=0, mib=8, in_hbm=0):
    def call(flags, *arrays):
        vmem = pl.BlockSpec(memory_space=pltpu.VMEM)
        return pl.pallas_call(
            kernel,
            out_shape=out_shapes,
            in_specs=[pl.BlockSpec(memory_space=pltpu.SMEM)]
            + [vmem] * (len(arrays) - in_hbm)
            + [pl.BlockSpec(memory_space=pltpu.HBM)] * in_hbm,
            out_specs=jax.tree.map(lambda _: vmem, out_shapes),
            scratch_shapes=list(scratch),
            compiler_params=pltpu.CompilerParams(vmem_limit_bytes=mib << 20),
            cost_estimate=pl.CostEstimate(
                flops=flops, bytes_accessed=moved, transcendentals=0
            ),
        )(flags, *arrays)

    return call


def flag(ref, name):
    return ref[FLAGS.index(name)]


def cols(at, size):
    return pl.ds(pl.multiple_of(at, BLOCK), size)


def copy_live(flags, rows, store):
    for r in range(0, rows, BLOCK):
        store(slice(r, r + BLOCK), r < flag(flags, "count"))


def masked(keep, x):
    return jnp.where(keep, x, jnp.zeros_like(x))


def pack_kernel(flags, hid, cot, sent_h, sent_c, own_c):
    half = cot.shape[1] // 2
    own = cols(flag(flags, "odd") * half, half)
    other = cols((1 - flag(flags, "odd")) * half, half)

    def store(r, live):
        sent_h[r, :] = masked(live, hid[r, :])
        sent_c[r, :] = masked(live, cot[r, other])
        own_c[r, :] = masked(live, cot[r, own])

    copy_live(flags, hid.shape[0], store)


def choose_kernel(name):
    def kernel(flags, yes, no, out):
        @pl.when(flag(flags, name) != 0)
        def _():
            out[...] = yes[...]

        @pl.when(flag(flags, name) == 0)
        def _():
            out[...] = no[...]

    return kernel


def export_kernel(flags, stored, partner_part, out):
    half = out.shape[1]

    @pl.when(flag(flags, "export_own") != 0)
    def _():
        out[...] = stored[:, cols(flag(flags, "odd") * half, half)]

    @pl.when(flag(flags, "export_own") == 0)
    def _():
        out[...] = partner_part[...]


def unit_kernel(flags, stored, partner_part, came, out):
    half = out.shape[1]
    begins = flag(flags, "begins") != 0
    paired = (flag(flags, "odd") != 0) & (flag(flags, "before_two") == 0)

    @pl.when(begins)
    def _():
        out[...] = stored[:, cols(flag(flags, "odd") * half, half)]

    @pl.when(jnp.logical_not(begins) & paired)
    def _():
        out[...] = partner_part[...]

    @pl.when(jnp.logical_not(begins | paired))
    def _():
        out[...] = came[...]


def grad_kernel(flags, own_h, own_c, core_h, core_c, from_h, from_c,
                t0, t1, t2, t3, near_h, near_c, ht, cs, sems):
    rows, units = own_h.shape
    copies = [
        pltpu.make_async_copy(from_h, near_h, sems.at[0]),
        pltpu.make_async_copy(from_c, near_c, sems.at[1]),
    ]
    for copy in copies:
        copy.start()
    cs[:rows, :] = own_c[...]
    cs[rows : 2 * rows, :] = masked(flag(flags, "partner") != 0, core_c[...])
    ht[:, :rows] = own_h[...].T
    ht[:, rows : 2 * rows] = core_h[...].T
    for copy in copies:
        copy.wait()
    ht[:, 2 * rows :] = near_h[...].T
    cs[2 * rows :, :] = masked(flag(flags, "helps") != 0, near_c[...])
    z = flag(flags, "z")
    quarter = units // 4
    for k, term in ((3, t3), (2, t2), (1, t1), (0, t0)):
        at = pl.multiple_of((z ^ k) * quarter, 16)
        term[...] = jnp.dot(
            ht[pl.ds(at, quarter), :], cs[...], preferred_element_type=F32
        ).astype(BF16)


def sum_kernel(flags, held, beside, crossed, relayed, *rest):
    outer, own, other = rest[:-2], rest[-2], rest[-1]
    none = jnp.zeros((), F32)
    place = flag(flags, "place")

    def pick(direct, passed, outside, ref):
        got = beside[...].astype(F32)
        got = jnp.where(place == direct, crossed[...].astype(F32), got)
        got = jnp.where(place == passed, relayed[...].astype(F32), got)
        if outer:
            got = jnp.where(place // 2 == outside, outer[ref][...].astype(F32), got)
        return got

    left, right = pick(4, 5, 0, 0), pick(3, 2, 3, 1)
    total = held[...].astype(F32)
    total = total + jnp.where(flag(flags, "before_two") != 0, left, none)
    total = total + jnp.where(flag(flags, "after_two") != 0, right, none)
    own[...] = total.astype(BF16)

    @pl.when(flag(flags, "partner") != 0)
    def _():
        other[...] = own[...]

    @pl.when(flag(flags, "partner") == 0)
    def _():
        odd = flag(flags, "odd") != 0
        theirs = jnp.where(odd, left, right)
        if outer:
            more = jnp.where(odd, outer[2][...].astype(F32), outer[3][...].astype(F32))
            theirs = theirs + jnp.where(flag(flags, "far_grad") != 0, more, none)
        other[...] = theirs.astype(BF16)


def forward_kernel(flags, own_h, own_c, core_h, core_c, near_h, near_c, u, a1, m1, a2, m2, a3,
                   out, hg, to_core, to_near, weight):
    units = own_h.shape[1]
    half = own_c.shape[1]
    z = flag(flags, "z")
    middle = (z == 1) | (z == 2)
    quarter = units // 4

    def place(k, value):
        at = pl.multiple_of((z ^ k) * quarter, 16)
        weight[pl.ds(at, quarter), :] = value

    place(0, u[...])
    place(1, a1[...])

    @pl.when(middle)
    def _():
        place(2, m2[...])
        place(3, m1[...])

    @pl.when(jnp.logical_not(middle))
    def _():
        place(2, a2[...])
        place(3, a3[...])

    w = weight[...]

    def products(h, c):
        o = jnp.dot(h, w, preferred_element_type=F32)
        g = lax.dot_general(c, w, (((1,), (1,)), ((), ())), preferred_element_type=F32)
        return o, g

    o, g = products(own_h[...], own_c[...])
    out[...] = o.astype(BF16)
    hg[...] = g
    for h, c, dst in ((core_h, core_c, to_core), (near_h, near_c, to_near)):
        o, g = products(h[...], c[...])
        dst[:, :half] = o.astype(BF16)
        dst[:, half:] = g.astype(BF16)


def output_kernel(flags, out, hg, core, near, output, hidden_grad):
    half = out.shape[1]
    odd = flag(flags, "odd")
    output[:, cols(odd * half, half)] = out[...]

    def finish(back):
        output[:, cols((1 - odd) * half, half)] = back[:, :half]
        hidden_grad[...] = (hg[...] + back[:, half:].astype(F32)).astype(BF16)

    @pl.when(flag(flags, "partner") != 0)
    def _():
        finish(core)

    @pl.when(flag(flags, "partner") == 0)
    def _():
        finish(near)


def join_kernel(flags, own, other, whole):
    half = own.shape[1]
    odd = flag(flags, "odd")
    whole[:, cols(odd * half, half)] = own[...]
    whole[:, cols((1 - odd) * half, half)] = other[...]


def make_body(n_ep, n_dp):
    assert n_dp == 4 and n_ep % 8 == 0
    both = ("ep", "dp")
    core_pairs = [(s, s ^ 1) for s in range(n_ep)]
    help_pairs = [(s, s + 1 if s % 2 else s - 1) for s in range(2, n_ep - 2)]
    back_pairs = [(b, a) for a, b in help_pairs]
    far = [(a, b) for a, b in help_pairs if {a % 8, b % 8} == {3, 4}]
    relays = {a ^ 5 for a, b in far}
    near = [(a, b) for a, b in help_pairs if (a, b) not in far]
    hop_one = [(a, a ^ 5) for a, b in far] + [p for p in near if p[0] in relays]
    hop_two = [(a ^ 5, b) for a, b in far] + [p for p in near if p[0] not in relays]
    by_one = {b for a, b in near if a in relays}
    right_two = [(s, s + 2) for s in range(n_ep - 2)]
    beside_pairs = [(s, s ^ 2) for s in range(n_ep)]
    moves = {2: 2, 5: -2, 3: 4, 4: -4}
    crossing = [(s, s + moves[s % 8]) for s in range(n_ep) if s % 8 in moves]
    relayed = [(s, s ^ 2) for s in range(n_ep) if s % 8 in (0, 7)]
    block_right = [(s, s + 2) for s in range(n_ep - 2) if s % 8 > 5]
    block_left = [(b, a) for a, b in block_right]
    right_four_weight = [(s - 4, s) for s in range(6, n_ep - 2, 2)]
    right_four_grad = [(s - 4, s) for s in range(7, n_ep - 2, 2)]
    left_four_grad = [(s + 4, s) for s in range(2, n_ep - 7, 2)]
    side_pairs = [(0, 1), (1, 0), (2, 3), (3, 2)]
    middle_pairs = []
    for s in range(n_ep):
        for z in range(n_dp):
            t, w = (s, z ^ 3) if z in (1, 2) else (s ^ 1, z)
            middle_pairs.append((s * n_dp + z, t * n_dp + w))

    def permute(x, axes, pairs):
        return lax.ppermute(x, axes, pairs) if pairs else jnp.zeros_like(x)

    def core(x):
        return permute(x, "ep", core_pairs)

    def shift(x, pairs):
        return permute(x, "ep", pairs)

    def side(x):
        return permute(x, "dp", side_pairs)

    def middle(x):
        return permute(x, both, middle_pairs)

    def plus(a, b):
        return (a.astype(F32) + b.astype(F32)).astype(BF16)

    def make_flags(slot_expert, count, s, z):
        places = lax.iota(jnp.int32, n_ep)
        odd = places % 2 == 1
        padded = jnp.pad(slot_expert, 4, constant_values=-1)
        e = {d: padded[4 + d : 4 + d + n_ep] for d in range(-4, 5)}
        eq = {d: e[d] == e[0] for d in e}
        partner = jnp.where(odd, eq[-1], eq[1])

        def among(members):
            found = places < 0
            for m in sorted(members):
                found = found | (places == m)
            return found

        rows = {
            "odd": odd,
            "z": z + 0 * places,
            "count": count + 0 * places,
            "partner": partner,
            "helps": jnp.where(odd, eq[1] & ~eq[2], eq[-1] & ~eq[-2]),
            "begins": ~eq[-1],
            "before_two": eq[-2],
            "after_two": eq[2],
            "export_own": partner != odd,
            "far_weight": eq[-3] & ~odd,
            "far_grad": jnp.where(odd, e[-4] == e[-1], e[4] == e[1]),
            "relay": among(relays),
            "by_one": among(by_one),
            "place": places % 8,
        }
        table = jnp.stack([rows[name].astype(jnp.int32) for name in FLAGS])
        return jnp.sum(jnp.where(places == s, table, 0), axis=1)

    def compute(hidden, cotangent, down_weight, slot_expert, row_counts):
        s = lax.axis_index("ep")
        z = lax.axis_index("dp")
        is_middle = (z == 1) | (z == 2)
        hid, cot, stored = hidden[0], cotangent[0], down_weight[0]
        capacity, units = hid.shape
        quarter, features = stored.shape
        half = features // 2
        flags = make_flags(slot_expert, row_counts[0, 0], s, z)

        def is_set(name):
            return flags[FLAGS.index(name)] != 0

        own_at = (s % 2) * half

        other_part = lax.dynamic_slice(stored, (0, half - own_at), (quarter, half))
        other_part, hid, cot = lax.optimization_barrier((other_part, hid, cot))
        own_part = lax.dynamic_slice(stored, (0, own_at), (quarter, half))
        piece = jax.ShapeDtypeStruct((quarter, half), BF16)
        h_piece = jax.ShapeDtypeStruct((capacity, units), BF16)
        c_piece = jax.ShapeDtypeStruct((capacity, half), BF16)
        packed = jax.ShapeDtypeStruct((capacity, units + half), BF16)
        wide = units + half
        small = 6 * quarter * half

        partner_part = core(other_part)
        export = local_kernel(export_kernel, piece, moved=small)(
            flags, stored, partner_part
        )
        came = shift(export, right_two)
        if right_four_weight:
            more = shift(export, right_four_weight)
            came = jnp.where(is_set("far_weight"), more, came)
        unit = local_kernel(unit_kernel, piece, moved=small)(
            flags, stored, partner_part, came
        )

        sent_h, sent_c, own_c = local_kernel(
            pack_kernel, [h_piece, c_piece, c_piece], moved=4 * capacity * wide
        )(flags, hid, cot)

        def to_neighbour(x):
            first = shift(x, hop_one)
            passed = local_kernel(choose_kernel("relay"), x, moved=4 * x.size)(
                flags, first, x
            )
            arrived = shift(passed, hop_two)
            if by_one:
                arrived = jnp.where(is_set("by_one"), first, arrived)
            return arrived

        near = [to_neighbour(sent_h), to_neighbour(sent_c)]
        from_core = [core(sent_h), core(sent_c)]
        *terms, near_h, near_c = local_kernel(
            grad_kernel,
            [piece] * 4 + [h_piece, c_piece],
            [
                pltpu.VMEM((units, 3 * capacity), BF16),
                pltpu.VMEM((3 * capacity, half), BF16),
                pltpu.SemaphoreType.DMA((2,)),
            ],
            flops=6 * capacity * units * half,
            moved=2 * units * half + 6 * capacity * wide,
            mib=16,
            in_hbm=2,
        )(flags, sent_h, own_c, *from_core, *near)

        a1 = side(unit)
        m1 = middle(unit)
        a2 = side(jnp.where(is_middle, m1, terms[3]))
        m2 = middle(a1)
        a3 = side(jnp.where(is_middle, m2, terms[2]))
        m3 = middle(plus(a2, terms[2]))
        last_side = jnp.where(is_middle, plus(m3, terms[1]), terms[1])
        last_middle = plus(a3, terms[3])
        last_side, last_middle, unit = lax.optimization_barrier(
            (last_side, last_middle, unit)
        )
        a4 = side(last_side)
        m4 = middle(last_middle)

        out, hg, to_core, to_next = local_kernel(
            forward_kernel,
            [
                jax.ShapeDtypeStruct((capacity, half), BF16),
                jax.ShapeDtypeStruct((capacity, units), F32),
                packed,
                packed,
            ],
            [pltpu.VMEM((units, half), BF16)],
            flops=12 * capacity * units * half,
            moved=2 * units * half + 12 * capacity * wide,
            mib=24,
        )(flags, sent_h, own_c, *from_core, near_h, near_c, unit, a1, m1, a2, m2, a3)
        a4, m4, to_core, to_next = lax.optimization_barrier((a4, m4, to_core, to_next))
        output, hidden_grad = local_kernel(
            output_kernel,
            [
                jax.ShapeDtypeStruct((capacity, features), BF16),
                jax.ShapeDtypeStruct((capacity, units), BF16),
            ],
            moved=8 * capacity * wide,
        )(flags, out, hg, core(to_core), shift(to_next, back_pairs))

        total = a4.astype(F32) + terms[0].astype(F32)
        total = total + jnp.where(is_middle, m4.astype(F32), 0.0)
        held = total.astype(BF16)
        crossed = shift(held, crossing)
        arrived = [shift(held, beside_pairs), crossed, shift(crossed, relayed)]
        if n_ep > 8:
            arrived += [
                shift(held, block_right),
                shift(held, block_left),
                shift(held, right_four_grad),
                shift(held, left_four_grad),
            ]
        group, other = local_kernel(sum_kernel, [piece, piece], moved=2 * small)(
            flags, held, *arrived
        )
        g = core(other)
        g, output, hidden_grad = lax.optimization_barrier((g, output, hidden_grad))
        weight_grad = local_kernel(
            join_kernel,
            jax.ShapeDtypeStruct((quarter, features), BF16),
            moved=4 * quarter * features,
        )(flags, group, g)
        return output[None], hidden_grad[None], weight_grad[None]

    return compute


def solution(mesh):
    spec = P("ep", "dp", None)
    return jax.shard_map(
        make_body(mesh.shape["ep"], mesh.shape["dp"]),
        mesh=mesh,
        in_specs=(spec, spec, spec, P(), P("ep", "dp")),
        out_specs=(spec, spec, spec),
        check_vma=False,
    )
```
